128 devices in a mesh: blk: 8 (over z_hi, x), seg: 16 (over z_lo, y, core).
Axes of the slice: x: 4, y: 4, z: 4 (z_hi: 2, z_lo: 2; z = z_hi * 2 + z_lo), core: 2. Of those that a mesh axis runs over, the one named last changes fastest.
Arguments:
- spectra: bfloat16 [16, 1024, 2, 4096], P(None, ('blk', 'seg')), may hold values from -6 to 6
- fibre_lists: int32 [16, 64], replicated, may hold values from 0 to 1023, as said below
- pairing: int32 [1, 16], replicated, may hold values from 0 to 15, as said below
Outputs:
- stack: float32 [1, 16, 64, 64, 128], P(None, 'blk', 'seg')
The draws below stay inside these ranges and needn't reach their ends.
Inputs may be any that keep to these rules, and one draw needn't show every extreme that they name: `fibre_lists`: row b lists the 64 channels of block b in an arbitrary order; every channel number appears exactly once in the table. Within every aligned range of 128 consecutive channel numbers, no block has more than 12 of its channels, and some block has exactly 12. `pairing`: row r maps every block to its partner in round r: the partner of the partner is the block itself, no block is its own partner, and no two rounds pair the same two blocks.
All inputs are finite; a program needn't handle non-finite values.
Results may differ from the reference program's by a relative error of at most 0.0037.
Values may be sent and summed in bfloat16 or wider, within the bound.
No kernel may reach another device: no remote copies, remote signals or barrier semaphores. Data moves between devices by JAX's collectives and lax.ppermute only.
A program may use at most 192 MiB of HBM per device.

```python
import math
import jax
import jax.numpy as jnp
from jax import lax

F = 4096
LH = 128
CH = 64
BLK_DEV = 2
ROUNDS = 1
NBLOCKS = 16
SEGMENTS = 16
CHANNELS = 1024
MOST = 12


def fibre_helper(key):
    columns = NBLOCKS // BLK_DEV
    width = BLK_DEV * CH
    keys = jax.random.split(key, 5)
    sigma = jax.random.permutation(keys[0], columns)
    shifts = jax.random.permutation(keys[1], NBLOCKS) % columns
    base = (CH - MOST) // (columns - 1)
    extra = (CH - MOST) % (columns - 1)
    weights = jnp.array([MOST] + [base + (1 if position < extra else 0) for position in range(columns - 1)], jnp.int32)
    for position in range(1, columns - 1, 2):
        limit = jnp.minimum(weights[position], MOST - weights[position + 1])
        moved = jax.random.randint(jax.random.fold_in(keys[2], position), (), 0, limit + 1)
        weights = weights.at[position].add(-moved).at[position + 1].add(moved)
    counts = weights[(sigma[:, None] - shifts[None, :]) % columns]
    ends = jnp.cumsum(counts, axis=1)
    places = jnp.arange(width, dtype=jnp.int32)
    block_at = jnp.sum((places[None, :, None] >= ends[:, None, :]).astype(jnp.int32), axis=2)
    orders = jax.vmap(lambda sub_key: jax.random.permutation(sub_key, width))(jax.random.split(keys[3], columns))
    block_of = jnp.zeros((columns, width), jnp.int32).at[jnp.arange(columns)[:, None], orders].set(block_at)
    flat_blocks = block_of.reshape(-1)
    numbers = jnp.arange(columns * width, dtype=jnp.int32)
    sort_keys = jnp.where(flat_blocks[None, :] == jnp.arange(NBLOCKS, dtype=jnp.int32)[:, None], numbers[None, :], columns * width)
    lists = jnp.sort(sort_keys, axis=1)[:, :CH]
    shuffles = jax.vmap(lambda sub_key: jax.random.permutation(sub_key, CH))(jax.random.split(keys[4], NBLOCKS))
    return jnp.take_along_axis(lists, shuffles, axis=1).astype(jnp.int32)


def draw_fibre_lists(key, part):
    return fibre_helper(jax.random.fold_in(key, 11))


def draw_pairing(key, part):
    circle = NBLOCKS - 1
    keys = jax.random.split(jax.random.fold_in(key, 23), 2)
    labels = jax.random.permutation(keys[0], NBLOCKS).astype(jnp.int32)
    chosen = jax.random.permutation(keys[1], circle)[:ROUNDS].astype(jnp.int32)
    blocks = jnp.arange(NBLOCKS, dtype=jnp.int32)

    def one_round(round_id):
        partner = jnp.where(blocks == circle, round_id, jnp.where(blocks == round_id, circle, (2 * round_id - blocks) % circle))
        return jnp.zeros((NBLOCKS,), jnp.int32).at[labels].set(labels[partner])
    return jax.vmap(one_round)(chosen).astype(jnp.int32)


def levels(own_key, extent, pieces, smallest, largest):
    def one(dim, parts):
        steps = jax.random.uniform(jax.random.fold_in(jax.random.fold_in(own_key, 6), dim), (parts,), jnp.float32, smallest / len(pieces), largest / len(pieces))
        return jnp.repeat(jnp.exp(steps), extent[dim] // parts).reshape((-1,) + (1,) * (len(extent) - dim - 1))

    factor_of = one(*pieces[0])
    for cut in pieces[1:]:
        factor_of = factor_of * one(*cut)
    return factor_of


def gaussian(key, dims, scale, reach, cuts=(), held_as=jnp.bfloat16):
    level = levels(key, dims, cuts, -0.22, 0.18) if cuts else 1.0
    result = jax.random.normal(key, dims, jnp.float32) * scale * level
    return jnp.minimum(jnp.maximum(result, -reach), reach).astype(held_as)


def setup_inputs(seed: int = 0) -> dict:
    key_list = jax.random.split(jax.random.key(seed), 4)
    spectra = gaussian(key_list[0], (SEGMENTS, CHANNELS, 2, F), 1.0, 6.0, ((1, 128),))
    fibre_lists = draw_fibre_lists(jax.random.fold_in(key_list[3], 71), 0)
    pairing = draw_pairing(jax.random.fold_in(key_list[3], 71), 0)
    return dict(spectra=spectra, fibre_lists=fibre_lists, pairing=pairing)


def make_table(frequencies, lag_count):
    freq_ids = jnp.arange(frequencies, dtype=jnp.int32)[:, None]
    lag_ids = jnp.arange(lag_count, dtype=jnp.int32)[None, :]
    angles = (freq_ids * lag_ids % (2 * frequencies)).astype(jnp.float32) * (math.pi / frequencies)
    return jnp.concatenate([jnp.cos(angles), -jnp.sin(angles)], 0).astype(jnp.bfloat16)

def cross_lags(left_rows, right_rows, lag_table):
    left_re = left_rows[:, 0].astype(jnp.float32)
    left_im = left_rows[:, 1].astype(jnp.float32)
    right_re = right_rows[:, 0].astype(jnp.float32)
    right_im = right_rows[:, 1].astype(jnp.float32)
    real_part = left_re[:, None, :] * right_re[None] + left_im[:, None, :] * right_im[None]
    imag_part = left_im[:, None, :] * right_re[None] - left_re[:, None, :] * right_im[None]
    spectrum = jnp.concatenate([real_part, imag_part], -1).astype(jnp.bfloat16)
    spectrum = spectrum.reshape(-1, spectrum.shape[-1])
    product = jnp.dot(spectrum, lag_table, preferred_element_type=jnp.float32)
    return product.reshape(left_rows.shape[0], right_rows.shape[0], -1)

def reference(spectra, fibre_lists, pairing):
    lag_table = make_table(F, LH)
    panels = jnp.take(spectra, fibre_lists.reshape(-1), axis=1).reshape(SEGMENTS, NBLOCKS, CH, 2, F)

    def unit_term(unit_index):
        round_id = unit_index // NBLOCKS
        block_id = unit_index % NBLOCKS
        partner = pairing[round_id, block_id]
        own_panel = lax.dynamic_index_in_dim(panels, block_id, 1, keepdims=False)
        other_panel = lax.dynamic_index_in_dim(panels, partner, 1, keepdims=False)

        def accumulate(step, running):
            left_rows = lax.dynamic_index_in_dim(own_panel, step, 0, keepdims=False)
            right_rows = lax.dynamic_index_in_dim(other_panel, step, 0, keepdims=False)
            return running + cross_lags(left_rows, right_rows, lag_table)
        return lax.fori_loop(0, SEGMENTS, accumulate, jnp.zeros((CH, CH, LH), jnp.float32))
    stacks = lax.map(unit_term, jnp.arange(ROUNDS * NBLOCKS, dtype=jnp.int32))
    return stacks.reshape(ROUNDS, NBLOCKS, CH, CH, LH) * (1.0 / math.sqrt(F * SEGMENTS))
```

```python
import functools
import math

import jax
import jax.numpy as jnp
from jax import lax
from jax.experimental import pallas as pl
from jax.experimental.pallas import tpu as pltpu
from jax.sharding import PartitionSpec as P

LH = 128
WIDE = 512


def make_tables(frequencies, lag_count):
    freq_ids = jnp.arange(frequencies, dtype=jnp.int32)[:, None]
    lag_ids = jnp.arange(lag_count, dtype=jnp.int32)[None, :]
    angles = (freq_ids * lag_ids % (2 * frequencies)).astype(jnp.float32) * (math.pi / frequencies)
    return jnp.cos(angles).astype(jnp.bfloat16), (-jnp.sin(angles)).astype(jnp.bfloat16)


def look_up(table, ids):
    hits = ids[:, None] == jnp.arange(table.shape[0], dtype=jnp.int32)[None, :]
    return jnp.sum(jnp.where(hits, table[None, :], 0), axis=1)


def choose_blocks(partner, blk_local):
    count = partner.shape[0]
    step = jnp.bitwise_xor(partner, 1)
    lowest = jnp.arange(count, dtype=jnp.int32)
    reach = 1
    while reach < count // blk_local:
        lowest = jnp.minimum(lowest, look_up(lowest, step))
        step = look_up(step, step)
        reach *= 2
    return 1 - jnp.bitwise_and(lowest, 1)


def pack_kernel(slot_ref, rows_ref, out_ref):
    sources, _, share, frequencies = rows_ref.shape
    dests, _, bound, _ = out_ref.shape
    shape = (dests * bound, sources * share)
    select = (lax.broadcasted_iota(jnp.int32, shape, 0) == slot_ref[...]).astype(jnp.bfloat16)

    def chunk(step, carry):
        span = pl.ds(pl.multiple_of(step * WIDE, WIDE), WIDE)
        for part in range(2):
            rows = rows_ref[:, part, :, span].astype(jnp.float32)
            rows = rows.reshape(sources * share, WIDE).astype(jnp.bfloat16)
            packed = jnp.dot(select, rows, preferred_element_type=jnp.float32)
            out_ref[:, part, :, span] = packed.reshape(dests, bound, WIDE).astype(jnp.bfloat16)
        return carry

    lax.fori_loop(0, frequencies // WIDE, chunk, 0)


def pair_kernel(group, wide, index_ref, rows_ref, cos_ref, sin_ref, own_ref, other_ref, x_re, x_im, y_re, y_im, sum_a, sum_b):
    sources, _, bound, frequencies = rows_ref.shape
    channels = x_re.shape[0]
    lags = cos_ref.shape[1]
    shares, _, share, _ = other_ref.shape
    shape = (2 * channels, sources * bound)
    select = (lax.broadcasted_iota(jnp.int32, shape, 1) == index_ref[...]).astype(jnp.bfloat16)

    def gather(step, carry):
        span = pl.ds(pl.multiple_of(step * WIDE, WIDE), WIDE)
        for part, x_out, y_out in ((0, x_re, y_re), (1, x_im, y_im)):
            rows = rows_ref[:, part, :, span].astype(jnp.float32)
            rows = rows.reshape(sources * bound, WIDE).astype(jnp.bfloat16)
            panel = jnp.dot(select, rows, preferred_element_type=jnp.float32)
            x_out[:, span] = panel[:channels]
            y_out[:, span] = panel[channels:].astype(y_out.dtype)
        return carry

    lax.fori_loop(0, frequencies // WIDE, gather, 0)

    def block(block_id, carry):
        sum_a[...] = jnp.zeros_like(sum_a)
        sum_b[...] = jnp.zeros_like(sum_b)

        def chunk(step, inner):
            span = pl.ds(pl.multiple_of(step * wide, wide), wide)
            real, imag = [], []
            right_re = [y_re[j : j + 16, span] for j in range(0, channels, 16)]
            right_im = [y_im[j : j + 16, span] for j in range(0, channels, 16)]
            for i in range(group):
                row = pl.ds(block_id * group + i, 1)
                left_re = jnp.broadcast_to(x_re[row, span], (16, wide)).astype(y_re.dtype)
                left_im = jnp.broadcast_to(x_im[row, span], (16, wide)).astype(y_re.dtype)
                for re, im in zip(right_re, right_im):
                    real.append((left_re * re + left_im * im).astype(jnp.bfloat16))
                    imag.append((left_im * re - left_re * im).astype(jnp.bfloat16))
            sum_a[...] += jnp.dot(jnp.concatenate(real, 0), cos_ref[span, :], preferred_element_type=jnp.float32)
            sum_b[...] += jnp.dot(jnp.concatenate(imag, 0), sin_ref[span, :], preferred_element_type=jnp.float32)
            return inner

        lax.fori_loop(0, frequencies // wide, chunk, 0)
        ahead = sum_a[...] + sum_b[...]
        back = (sum_a[...] - sum_b[...]).reshape(group, shares, share, lags)
        own_ref[pl.ds(block_id * group, group)] = ahead.astype(jnp.bfloat16).reshape(group, channels, lags)
        for i in range(group):
            other_ref[:, block_id * group + i] = back[i].astype(jnp.bfloat16)
        return carry

    lax.fori_loop(0, channels // group, block, 0)


def in_vmem(count):
    return [pl.BlockSpec(memory_space=pltpu.VMEM)] * count


def local(spectra, fibre_lists, pairing):
    frequencies = spectra.shape[-1]
    blk_count = lax.axis_size("blk")
    seg_count = lax.axis_size("seg")
    blk_index = lax.axis_index("blk")
    block_count, channels = fibre_lists.shape
    blk_local = block_count // blk_count
    width = blk_local * channels
    side_rows = 3 * channels // (2 * blk_count)
    bound = 2 * side_rows
    share = channels // seg_count

    planar = jnp.transpose(spectra, (0, 2, 1, 3))
    column = lax.all_to_all(planar, "seg", split_axis=0, concat_axis=0, tiled=True)

    partner = pairing[0]
    blocks = jnp.arange(block_count, dtype=jnp.int32)
    chosen = choose_blocks(partner, blk_local)
    worker = jnp.where(chosen == 1, blocks, partner) // blk_local
    source = fibre_lists // width
    earlier = jnp.arange(channels)[None, :] < jnp.arange(channels)[:, None]
    same = (source[:, :, None] == source[:, None, :]) & earlier[None]
    rank = jnp.sum(same.astype(jnp.int32), axis=2)
    side_slot = (1 - chosen)[:, None] * side_rows + rank
    target = worker[:, None] * bound + side_slot
    numbers = blk_index * width + jnp.arange(width, dtype=jnp.int32)
    found = fibre_lists.reshape(-1)[:, None] == numbers[None, :]
    send_slot = jnp.sum(jnp.where(found, target.reshape(-1)[:, None], 0), axis=0)

    own_first = blk_index * blk_local
    own_block = own_first + jnp.sum(jnp.where(blocks == own_first, 1 - chosen, 0))
    other_block = jnp.sum(jnp.where(blocks == own_block, partner, 0))
    arrived_slot = source * bound + side_slot
    wanted = jnp.stack([own_block, other_block])[:, None] == blocks[None, :]
    index = jnp.sum(jnp.where(wanted[:, :, None], arrived_slot[None], 0), axis=1).reshape(-1, 1)

    packed = pl.pallas_call(
        pack_kernel,
        out_shape=jax.ShapeDtypeStruct((blk_count, 2, bound, frequencies), jnp.bfloat16),
        in_specs=in_vmem(2),
        out_specs=in_vmem(1)[0],
        compiler_params=pltpu.CompilerParams(vmem_limit_bytes=24 * 2**20),
    )(send_slot.reshape(1, width), column)
    arrived = lax.all_to_all(packed, "blk", split_axis=0, concat_axis=0, tiled=True)

    cos_table, sin_table = make_tables(frequencies, LH)
    group, wide = 16, 512
    own_part, other_part = pl.pallas_call(
        functools.partial(pair_kernel, group, wide),
        out_shape=[
            jax.ShapeDtypeStruct((channels, channels, LH), jnp.bfloat16),
            jax.ShapeDtypeStruct((seg_count, channels, share, LH), jnp.bfloat16),
        ],
        in_specs=in_vmem(4),
        out_specs=in_vmem(2),
        scratch_shapes=[pltpu.VMEM((channels, frequencies), jnp.float32)] * 4
        + [pltpu.VMEM((group * channels, LH), jnp.float32)] * 2,
        compiler_params=pltpu.CompilerParams(vmem_limit_bytes=40 * 2**20),
    )(index, arrived, cos_table, sin_table)

    scaling = 1.0 / math.sqrt(frequencies * seg_count)
    other_sums = lax.all_to_all(other_part, "seg", split_axis=0, concat_axis=0, tiled=True)
    other_rows = jnp.sum(other_sums.astype(jnp.float32), axis=0) * scaling
    other_rows = jnp.transpose(other_rows, (1, 0, 2)).astype(jnp.bfloat16)
    own_part = own_part.reshape(seg_count, share, channels, LH)
    own_sums = lax.all_to_all(own_part, "seg", split_axis=0, concat_axis=0, tiled=True)
    own_rows = jnp.sum(own_sums.astype(jnp.float32), axis=0) * scaling

    everyone = jnp.broadcast_to(other_rows[None], (blk_count,) + other_rows.shape)
    offered = lax.all_to_all(everyone, "blk", split_axis=0, concat_axis=0, tiled=True)
    lacking = 2 * own_first + blk_local - 1 - own_block
    giver = jnp.sum(jnp.where(blocks == lacking, worker, 0))
    taken = lax.dynamic_index_in_dim(offered, giver, 0, keepdims=False).astype(jnp.float32)
    own_is_first = own_block == own_first
    first = jnp.where(own_is_first, own_rows, taken)
    second = jnp.where(own_is_first, taken, own_rows)
    return jnp.stack([first, second])[None]


def solution(mesh):
    in_specs = (P(None, ("blk", "seg"), None, None), P(), P())
    out_specs = P(None, "blk", "seg", None, None)
    return jax.shard_map(local, mesh=mesh, in_specs=in_specs, out_specs=out_specs, check_vma=False)
```

```python
import functools
import math

import jax
import jax.numpy as jnp
from jax import lax
from jax.experimental import pallas as pl
from jax.experimental.pallas import tpu as pltpu
from jax.sharding import PartitionSpec as P

LH = 128


def make_table(frequencies, first, count, lag_count):
    freq_ids = first + jnp.arange(count, dtype=jnp.int32)[:, None]
    lag_ids = jnp.arange(lag_count, dtype=jnp.int32)[None, :]
    angles = (freq_ids * lag_ids % (2 * frequencies)).astype(jnp.float32) * (math.pi / frequencies)
    return jnp.concatenate([jnp.cos(angles), -jnp.sin(angles)], 1).astype(jnp.bfloat16)


def look_up(table, ids):
    hits = ids[:, None] == jnp.arange(table.shape[0], dtype=jnp.int32)[None, :]
    return jnp.sum(jnp.where(hits, table[None, :], 0), axis=1)


def choose_blocks(partner, blk_local):
    count = partner.shape[0]
    step = jnp.bitwise_xor(partner, 1)
    lowest = jnp.arange(count, dtype=jnp.int32)
    reach = 1
    while reach < count // blk_local:
        lowest = jnp.minimum(lowest, look_up(lowest, step))
        step = look_up(step, step)
        reach *= 2
    return 1 - jnp.bitwise_and(lowest, 1)


def rows_of(ref, *at):
    part = ref[(slice(None),) + at].astype(jnp.float32)
    return part.reshape(part.shape[0] * part.shape[1], part.shape[2]).astype(jnp.bfloat16)


def dot(left, right):
    return jnp.dot(left, right, preferred_element_type=jnp.float32)


def dot_rows(left, right):
    return lax.dot_general(left, right, (((1,), (1,)), ((), ())), preferred_element_type=jnp.float32)


def pack_kernel(slot_ref, rows_ref, out_ref, staged, sent):
    sources, segments, parts, share, _ = rows_ref.shape
    dests, _, _, bound, size = out_ref.shape
    shape = (dests * bound, sources * share)
    select = (lax.broadcasted_iota(jnp.int32, shape, 0) == slot_ref[...]).astype(jnp.bfloat16)

    def copy_out(step):
        return pltpu.make_async_copy(staged.at[step], out_ref.at[:, step], sent.at[step])

    def segment(step, carry):
        for part in range(parts):
            packed = dot(select, rows_of(rows_ref, step, part))
            staged[step, :, part] = packed.reshape(dests, bound, size).astype(jnp.bfloat16)
        copy_out(step).start()
        return carry

    lax.fori_loop(0, segments, segment, 0, unroll=4)
    for step in range(segments):
        copy_out(step).wait()


def pair_kernel(batch, group, index_ref, rows_ref, table_ref, message_ref, series, spectrum):
    sources, segments, parts, bound, band = rows_ref.shape
    terms = parts * segments
    shares, quads, share, lags = message_ref.shape
    channels = quads // 2
    both = 2 * channels
    shape = (both, sources * bound)
    select = (lax.broadcasted_iota(jnp.int32, shape, 1) == index_ref[...]).astype(jnp.bfloat16)

    def unit(rows, columns, shift):
        row = lax.broadcasted_iota(jnp.int32, (rows, columns), 0)
        column = lax.broadcasted_iota(jnp.int32, (rows, columns), 1)
        return (row + shift == column).astype(jnp.bfloat16)

    turn_band = unit(band, band, 0)
    pick_left = unit(channels, both, channels)
    turn_both = unit(both, both, 0)

    def segment(step, carry):
        for part in range(parts):
            panel = dot(select, rows_of(rows_ref, step, part)).astype(jnp.bfloat16)
            series[pl.ds(part * segments + step, band, stride=terms + 8), :] = dot_rows(turn_band, panel)
        return carry

    lax.fori_loop(0, segments, segment, 0, unroll=4)

    low = lax.broadcasted_iota(jnp.int32, (batch * terms, both), 1) < channels
    term_of = lax.broadcasted_iota(jnp.int32, (channels, batch * terms), 1) // terms

    def frequencies(step, carry):
        starts = [pl.multiple_of((step * batch + f) * (terms + 8), 8) for f in range(batch)]
        block = jnp.concatenate([series[pl.ds(start, terms), :] for start in starts], 0)
        left = dot_rows(pick_left, block.astype(jnp.bfloat16))
        lefts = [jnp.where(term_of == f, left, 0.0).astype(jnp.bfloat16) for f in range(batch)]
        turned = []
        for f in range(batch):
            turned += [-block[f * terms + segments : (f + 1) * terms], block[f * terms : f * terms + segments]]
        turned = pltpu.roll(jnp.concatenate(turned, 0), channels, axis=1)
        right = jnp.where(low, block, turned).astype(jnp.bfloat16)
        crossed = dot(jnp.concatenate(lefts, 0), right)
        for f in range(batch):
            where = pl.ds(pl.multiple_of((step * batch + f) * (channels + 8), 8), channels)
            spectrum[where, :] = crossed[f * channels : (f + 1) * channels]
        return carry

    lax.fori_loop(0, band // batch, frequencies, 0, unroll=8)
    strips = channels // share
    kept = channels // shares

    def lag_rows(step, carry):
        lines = []
        for i in range(group):
            line = spectrum[pl.ds(step * group + i, band, stride=channels + 8), :]
            lines.append(dot_rows(turn_both, line.astype(jnp.bfloat16)).astype(jnp.bfloat16))
        sums = dot(jnp.concatenate(lines, 0), table_ref[...])
        for i in range(group):
            real = sums[i * both : i * both + channels, :lags]
            imag = sums[i * both + channels : (i + 1) * both, lags:]
            ahead = (real + imag).reshape(strips, share, lags).astype(jnp.bfloat16)
            back = (real - imag).reshape(shares, share, lags).astype(jnp.bfloat16)
            row = step * group + i
            message_ref[row // kept, pl.ds((row % kept) * strips, strips)] = ahead
            message_ref[:, channels + row] = back
        return carry

    lax.fori_loop(0, channels // group, lag_rows, 0)


def in_vmem(count):
    return [pl.BlockSpec(memory_space=pltpu.VMEM)] * count


def local(spectra, fibre_lists, pairing):
    frequencies = spectra.shape[-1]
    blk_count = lax.axis_size("blk")
    seg_count = lax.axis_size("seg")
    blk_index = lax.axis_index("blk")
    block_count, channels = fibre_lists.shape
    blk_local = block_count // blk_count
    width = blk_local * channels
    side_rows = 3 * channels // (2 * blk_count)
    bound = 2 * side_rows
    share = channels // seg_count
    segments, holders, parts, _ = spectra.shape
    band = frequencies // seg_count
    bands = spectra.reshape(segments, holders, parts, seg_count, band)
    bands = jnp.transpose(bands, (3, 0, 2, 1, 4))
    column = lax.all_to_all(bands, "seg", split_axis=0, concat_axis=0, tiled=True)

    partner = pairing[0]
    blocks = jnp.arange(block_count, dtype=jnp.int32)
    chosen = choose_blocks(partner, blk_local)
    worker = jnp.where(chosen == 1, blocks, partner) // blk_local
    source = fibre_lists // width
    earlier = jnp.arange(channels)[None, :] < jnp.arange(channels)[:, None]
    same = (source[:, :, None] == source[:, None, :]) & earlier[None]
    rank = jnp.sum(same.astype(jnp.int32), axis=2)
    side_slot = (1 - chosen)[:, None] * side_rows + rank
    target = worker[:, None] * bound + side_slot
    numbers = blk_index * width + jnp.arange(width, dtype=jnp.int32)
    found = fibre_lists.reshape(-1)[:, None] == numbers[None, :]
    send_slot = jnp.sum(jnp.where(found, target.reshape(-1)[:, None], 0), axis=0).reshape(1, width)

    own_first = blk_index * blk_local
    own_block = own_first + jnp.sum(jnp.where(blocks == own_first, 1 - chosen, 0))
    other_block = jnp.sum(jnp.where(blocks == own_block, partner, 0))
    arrived_slot = source * bound + side_slot
    wanted = jnp.stack([other_block, own_block])[:, None] == blocks[None, :]
    index = jnp.sum(jnp.where(wanted[:, :, None], arrived_slot[None], 0), axis=1)
    index = index.reshape(2 * channels, 1)

    packed = pl.pallas_call(
        pack_kernel,
        out_shape=pltpu.HBM((blk_count, segments, parts, bound, band), jnp.bfloat16),
        in_specs=in_vmem(2),
        out_specs=pl.BlockSpec(memory_space=pltpu.HBM),
        scratch_shapes=[
            pltpu.VMEM((segments, blk_count, parts, bound, band), jnp.bfloat16),
            pltpu.SemaphoreType.DMA((segments,)),
        ],
        compiler_params=pltpu.CompilerParams(vmem_limit_bytes=16 * 2**20),
    )(send_slot, column)
    arrived = lax.all_to_all(packed, "blk", split_axis=0, concat_axis=0, tiled=True)

    table = make_table(frequencies, lax.axis_index("seg") * band, band, LH)
    message = pl.pallas_call(
        functools.partial(pair_kernel, 8, 16),
        out_shape=jax.ShapeDtypeStruct((seg_count, 2 * channels, share, LH), jnp.bfloat16),
        in_specs=in_vmem(3),
        out_specs=in_vmem(1)[0],
        scratch_shapes=[
            pltpu.VMEM((band * (parts * segments + 8), 2 * channels), jnp.float32),
            pltpu.VMEM((band * (channels + 8), 2 * channels), jnp.float32),
        ],
        compiler_params=pltpu.CompilerParams(vmem_limit_bytes=40 * 2**20),
    )(index, arrived, table)

    scaling = 1.0 / math.sqrt(frequencies * segments)
    received = lax.all_to_all(message, "seg", split_axis=0, concat_axis=0, tiled=True)
    total = jnp.sum(received.astype(jnp.float32), axis=0) * scaling
    own = total[:channels].reshape(share, channels, LH)
    other = jnp.transpose(total[channels:], (1, 0, 2)).astype(jnp.bfloat16)
    everyone = jnp.broadcast_to(other[None], (blk_count,) + other.shape)
    offered = lax.all_to_all(everyone, "blk", split_axis=0, concat_axis=0, tiled=True)

    lacking = 2 * own_first + blk_local - 1 - own_block
    giver = jnp.sum(jnp.where(blocks == lacking, worker, 0))
    taken = lax.dynamic_index_in_dim(offered, giver, 0, keepdims=False).astype(jnp.float32)
    own_is_first = own_block == own_first
    first = jnp.where(own_is_first, own, taken)
    second = jnp.where(own_is_first, taken, own)
    return jnp.stack([first, second])[None]


def solution(mesh):
    in_specs = (P(None, ("blk", "seg"), None, None), P(), P())
    out_specs = P(None, "blk", "seg", None, None)
    return jax.shard_map(local, mesh=mesh, in_specs=in_specs, out_specs=out_specs, check_vma=False)
```

```python
import functools
import math

import jax
import jax.numpy as jnp
from jax import lax
from jax.experimental import pallas as pl
from jax.experimental.pallas import tpu as pltpu
from jax.sharding import PartitionSpec as P


LH = 128
SHARES = (6, 10)
TURNS = (5, 7, 4, 6, 2, 3, 1)


def make_table(frequencies, first, count, lag_count):
    freq_ids = first + jnp.arange(count, dtype=jnp.int32)[:, None]
    lag_ids = jnp.arange(lag_count, dtype=jnp.int32)[None, :]
    angles = (freq_ids * lag_ids % (2 * frequencies)).astype(jnp.float32) * (math.pi / frequencies)
    return jnp.concatenate([jnp.cos(angles), -jnp.sin(angles)], 1).astype(jnp.bfloat16)


def look_up(table, ids):
    hits = ids[:, None] == jnp.arange(table.shape[0], dtype=jnp.int32)[None, :]
    return jnp.sum(jnp.where(hits, table[None, :], 0), axis=1)


def turn_of(to, start, ring):
    return (to // ring - start // ring) % 2 * ring + (to - start) % ring


def choose_blocks(partner, blk_local):
    count = partner.shape[0]
    step = jnp.bitwise_xor(partner, 1)
    lowest = jnp.arange(count, dtype=jnp.int32)
    reach = 1
    while reach < count // blk_local:
        lowest = jnp.minimum(lowest, look_up(lowest, step))
        step = look_up(step, step)
        reach *= 2
    return 1 - jnp.bitwise_and(lowest, 1)


def stacked(parts):
    rows = jnp.concatenate([part.astype(jnp.float32) for part in parts], 0)
    return rows.astype(jnp.bfloat16)


def dot(left, right):
    return jnp.dot(left, right, preferred_element_type=jnp.float32)


def dot_rows(left, right):
    return lax.dot_general(left, right, (((1,), (1,)), ((), ())), preferred_element_type=jnp.float32)


def pack_kernel(slot_ref, rows_ref, *out_refs):
    sources, segments, parts, share, _ = rows_ref.shape
    bound = out_refs[0].shape[2]
    shape = (len(out_refs) * bound, sources * share)
    select = (lax.broadcasted_iota(jnp.int32, shape, 0) == slot_ref[...]).astype(jnp.bfloat16)

    def segment(step, carry):
        for part in range(parts):
            rows = stacked([rows_ref[source, step, part] for source in range(sources)])
            packed = dot(select, rows).astype(jnp.bfloat16)
            for turn, out_ref in enumerate(out_refs):
                out_ref[step, part] = packed[turn * bound : (turn + 1) * bound]
        return carry

    lax.fori_loop(0, segments, segment, 0, unroll=segments // 2)


def pair_kernel(batch, group, index_ref, table_ref, *refs):
    rows_refs, (message_ref, series, spectrum) = refs[:-3], refs[-3:]
    _, parts, bound, band = rows_refs[0].shape
    sources = len(rows_refs) // len(SHARES)
    groups = [rows_refs[first : first + sources] for first in range(0, len(rows_refs), sources)]
    segments = sum(held[0].shape[0] for held in groups)
    terms = parts * segments
    shares, quads, share, lags = message_ref.shape
    channels = quads // 2
    both = 2 * channels
    shape = (both, sources * bound)
    select = (lax.broadcasted_iota(jnp.int32, shape, 1) == index_ref[...]).astype(jnp.bfloat16)

    def unit(rows, columns, shift):
        row = lax.broadcasted_iota(jnp.int32, (rows, columns), 0)
        column = lax.broadcasted_iota(jnp.int32, (rows, columns), 1)
        return (row + shift == column).astype(jnp.bfloat16)

    turn_band = unit(band, band, 0)
    pick_left = unit(channels, both, channels)
    turn_both = unit(both, both, 0)

    before = 0
    for held in groups:

        def segment(step, carry, before=before, held=held):
            for part in range(parts):
                panel = dot(select, stacked([ref[step, part] for ref in held])).astype(jnp.bfloat16)
                first = part * segments + before + step
                series[pl.ds(first, band, stride=terms + 8), :] = dot_rows(turn_band, panel)
            return carry

        each = held[0].shape[0]
        lax.fori_loop(0, each, segment, 0, unroll=each // 2)
        before += each

    low = lax.broadcasted_iota(jnp.int32, (batch * terms, both), 1) < channels
    term_of = lax.broadcasted_iota(jnp.int32, (channels, batch * terms), 1) // terms

    def frequencies(step, carry):
        starts = [pl.multiple_of((step * batch + f) * (terms + 8), 8) for f in range(batch)]
        block = jnp.concatenate([series[pl.ds(start, terms), :] for start in starts], 0)
        left = dot_rows(pick_left, block.astype(jnp.bfloat16))
        lefts = [jnp.where(term_of == f, left, 0.0).astype(jnp.bfloat16) for f in range(batch)]
        turned = []
        for f in range(batch):
            turned += [-block[f * terms + segments : (f + 1) * terms], block[f * terms : f * terms + segments]]
        turned = pltpu.roll(jnp.concatenate(turned, 0), channels, axis=1)
        right = jnp.where(low, block, turned).astype(jnp.bfloat16)
        crossed = dot(jnp.concatenate(lefts, 0), right)
        for f in range(batch):
            where = pl.ds(pl.multiple_of((step * batch + f) * (channels + 8), 8), channels)
            spectrum[where, :] = crossed[f * channels : (f + 1) * channels]
        return carry

    lax.fori_loop(0, band // batch, frequencies, 0, unroll=8)
    strips = channels // share
    kept = channels // shares

    def lag_rows(step, carry):
        lines = []
        for i in range(group):
            line = spectrum[pl.ds(step * group + i, band, stride=channels + 8), :]
            lines.append(dot_rows(turn_both, line.astype(jnp.bfloat16)).astype(jnp.bfloat16))
        sums = dot(jnp.concatenate(lines, 0), table_ref[...])
        for i in range(group):
            real = sums[i * both : i * both + channels, :lags]
            imag = sums[i * both + channels : (i + 1) * both, lags:]
            ahead = (real + imag).reshape(strips, share, lags).astype(jnp.bfloat16)
            back = (real - imag).reshape(shares, share, lags).astype(jnp.bfloat16)
            row = step * group + i
            message_ref[row // kept, pl.ds((row % kept) * strips, strips)] = ahead
            message_ref[:, channels + row] = back
        return carry

    lax.fori_loop(0, channels // group, lag_rows, 0)


def in_vmem(count):
    return [pl.BlockSpec(memory_space=pltpu.VMEM)] * count


def stacks(spectra, fibre_lists, pairing):
    frequencies = spectra.shape[-1]
    blk_count = lax.axis_size("blk")
    seg_count = lax.axis_size("seg")
    blk_index = lax.axis_index("blk")
    block_count, channels = fibre_lists.shape
    blk_local = block_count // blk_count
    width = blk_local * channels
    ring = blk_count // 2
    side_rows = 3 * channels // (2 * blk_count)
    bound = 2 * side_rows
    share = channels // seg_count
    segments, holders, parts, _ = spectra.shape
    band = frequencies // seg_count
    sizes = [segments * part // sum(SHARES) for part in SHARES]
    columns, first = [], 0
    for size in sizes:
        bands = spectra[first : first + size].reshape(size, holders, parts, seg_count, band)
        bands = jnp.transpose(bands, (3, 0, 2, 1, 4))
        columns.append(lax.all_to_all(bands, "seg", split_axis=0, concat_axis=0, tiled=True))
        first += size

    partner = pairing[0]
    blocks = jnp.arange(block_count, dtype=jnp.int32)
    chosen = choose_blocks(partner, blk_local)
    worker = jnp.where(chosen == 1, blocks, partner) // blk_local
    source = fibre_lists // width
    earlier = jnp.arange(channels)[None, :] < jnp.arange(channels)[:, None]
    same = (source[:, :, None] == source[:, None, :]) & earlier[None]
    rank = jnp.sum(same.astype(jnp.int32), axis=2)
    side_slot = (1 - chosen)[:, None] * side_rows + rank
    target = turn_of(worker, blk_index, ring)[:, None] * bound + side_slot
    numbers = blk_index * width + jnp.arange(width, dtype=jnp.int32)
    found = fibre_lists.reshape(-1)[:, None] == numbers[None, :]
    send_slot = jnp.sum(jnp.where(found, target.reshape(-1)[:, None], 0), axis=0).reshape(1, width)

    own_first = blk_index * blk_local
    own_block = own_first + jnp.sum(jnp.where(blocks == own_first, 1 - chosen, 0))
    other_block = jnp.sum(jnp.where(blocks == own_block, partner, 0))
    arrived_slot = turn_of(blk_index, source, ring) * bound + side_slot
    wanted = jnp.stack([other_block, own_block])[:, None] == blocks[None, :]
    index = jnp.sum(jnp.where(wanted[:, :, None], arrived_slot[None], 0), axis=1)
    index = index.reshape(2 * channels, 1)

    arrived = []
    turned = []
    for turn in range(blk_count):
        moves = [(k // ring + turn // ring) % 2 * ring + (k + turn) % ring for k in range(blk_count)]
        turned.append(list(enumerate(moves)))
    for size, column in zip(sizes, columns):
        piece = jax.ShapeDtypeStruct((size, parts, bound, band), jnp.bfloat16)
        pack = pl.pallas_call(
            pack_kernel,
            out_shape=[piece] * blk_count,
            in_specs=in_vmem(2),
            out_specs=in_vmem(blk_count),
            compiler_params=pltpu.CompilerParams(vmem_limit_bytes=16 * 2**20),
        )
        packed = pack(send_slot, column)
        pieces = list(packed)
        for turn in TURNS:
            pieces[turn] = lax.ppermute(packed[turn], "blk", turned[turn])
        arrived += pieces

    table = make_table(frequencies, lax.axis_index("seg") * band, band, LH)
    message = pl.pallas_call(
        functools.partial(pair_kernel, 8, 16),
        out_shape=jax.ShapeDtypeStruct((seg_count, 2 * channels, share, LH), jnp.bfloat16),
        in_specs=in_vmem(2 + len(arrived)),
        out_specs=in_vmem(1)[0],
        scratch_shapes=[
            pltpu.VMEM((band * (parts * segments + 8), 2 * channels), jnp.float32),
            pltpu.VMEM((band * (channels + 8), 2 * channels), jnp.float32),
        ],
        compiler_params=pltpu.CompilerParams(vmem_limit_bytes=40 * 2**20),
    )(index, table, *arrived)

    scaling = 1.0 / math.sqrt(frequencies * segments)
    received = lax.all_to_all(message, "seg", split_axis=0, concat_axis=0, tiled=True)
    total = jnp.sum(received.astype(jnp.float32), axis=0) * scaling
    own = total[:channels].reshape(share, channels, LH)
    other = jnp.transpose(total[channels:], (1, 0, 2)).astype(jnp.bfloat16)
    everyone = jnp.broadcast_to(other[None], (blk_count,) + other.shape)
    offered = lax.all_to_all(everyone, "blk", split_axis=0, concat_axis=0, tiled=True)

    lacking = 2 * own_first + blk_local - 1 - own_block
    giver = jnp.sum(jnp.where(blocks == lacking, worker, 0))
    taken = lax.dynamic_index_in_dim(offered, giver, 0, keepdims=False).astype(jnp.float32)
    own_is_first = own_block == own_first
    first = jnp.where(own_is_first, own, taken)
    second = jnp.where(own_is_first, taken, own)
    return jnp.stack([first, second])[None]


def solution(mesh):
    in_specs = (P(None, ("blk", "seg"), None, None), P(), P())
    out_specs = P(None, "blk", "seg", None, None)
    return jax.shard_map(stacks, mesh=mesh, in_specs=in_specs, out_specs=out_specs, check_vma=False)
```
